32 devices in a mesh: leaf: 2 (over core), blk: 4 (over y, x), col: 4 (over z).
Axes of the slice: x: 2, y: 2, z: 4, core: 2. Of those that a mesh axis runs over, the one named last changes fastest.
Arguments:
- front_sizes: int32 [2], replicated, may hold values from 1024 to 2048, as said below
- unit_rows: int32 [512], P('col'), may hold values from 0 to 4095, as said below
- target_rows: int32 [32, 512], P(None, 'col'), may hold values from 0 to 2047, as said below
- leaf_inverse: bfloat16 [4096, 2048], P(('leaf', 'blk')), may hold values from -0.125 to 0.125
- leaf_coupling: bfloat16 [256, 4096], P(None, ('leaf', 'blk')), may hold values from -0.59765625 to 0.59765625
- sep_factor: bfloat16 [256, 256], P(('leaf', 'blk'))
Outputs:
- entries: float32 [32, 512], P(('leaf', 'blk'), 'col')
The draws below stay inside these ranges and needn't reach their ends.
Inputs may be any that keep to these rules, and one draw needn't show every extreme that they name: `front_sizes`: one leaf has exactly 2048 live rows. The offset of each unit (unit_rows mod 2048) is below the front size of its leaf. `target_rows`: each offset lies in the front of the leaf that holds the column's unit, padding rows included.
All inputs are finite; a program needn't handle non-finite values.
Results may differ from the reference program's by a relative error of at most 0.014.
Values sent between devices are 32-bit elements; how exact they have to be, the bound alone decides.
A program may use at most 64 MiB of HBM per device.

```python
import jax
import jax.numpy as jnp
from jax import lax

LEAF = 2048
SEP = 256
LEVELS = 1
PANEL = 512
SEPSUM = 256
CPLW = 0
TGT = 32
N_LEAF = 2


def front_table(key):
    base = jax.random.fold_in(key, 7001)
    widths = jax.random.randint(jax.random.fold_in(base, 1), (N_LEAF,), LEAF // 2, LEAF + 1)
    chosen = jax.random.randint(jax.random.fold_in(base, 2), (), 0, N_LEAF)
    return jnp.where(jnp.arange(N_LEAF) == chosen, LEAF, widths).astype(jnp.int32)


def unit_table(key):
    widths = front_table(key)
    base = jax.random.fold_in(key, 7002)
    first = jax.random.randint(jax.random.fold_in(base, 1), (PANEL,), 0, N_LEAF)
    second = jax.random.randint(jax.random.fold_in(base, 2), (PANEL,), 0, N_LEAF)
    rotate = jax.random.randint(jax.random.fold_in(base, 3), (), 0, N_LEAF)
    leaves = (jnp.minimum(first, second) + rotate) % N_LEAF
    limits = widths[leaves]
    offsets = jax.random.randint(jax.random.fold_in(base, 4), (PANEL,), 0, limits)
    return (leaves, offsets, limits)


def draw_front_sizes(key, part):
    return front_table(key)


def draw_unit_rows(key, part):
    leaves, offsets, limits = unit_table(key)
    return (leaves * LEAF + offsets).astype(jnp.int32)


def draw_target_rows(key, part):
    leaves, offsets, limits = unit_table(key)
    base = jax.random.fold_in(key, 7003)
    padded = jax.random.randint(jax.random.fold_in(base, 1), (PANEL,), 0, 4) == 0
    reach = jnp.where(padded, LEAF, limits)
    return jax.random.randint(jax.random.fold_in(base, 2), (TGT, PANEL), 0, reach[None, :]).astype(jnp.int32)


def draw_sep_factor(key, part):
    width = SEPSUM + CPLW
    places = jnp.arange(width)
    scales = jnp.full((width,), 0.1, jnp.float32)
    for level in range(1, LEVELS + 1):
        lowest = SEP * (2 ** (level - 1) - 1)
        highest = SEP * (2 ** level - 1)
        inside = (places >= lowest) & (places < highest)
        scales = jnp.where(inside, (SEP * 2 ** (level - 1)) ** (-0.5), scales)
    shape = (N_LEAF * SEP // 2, width)
    values = jax.random.normal(jax.random.fold_in(key, 7005), shape, jnp.float32)
    return (values * scales[None, :]).astype(jnp.bfloat16)


def steps_of(own_key, dims, cuts, least, largest):
    def one(axis_at, parts):
        draws = jax.random.uniform(jax.random.fold_in(jax.random.fold_in(own_key, 6), axis_at), (parts,), jnp.float32, least / len(cuts), largest / len(cuts))
        return jnp.repeat(jnp.exp(draws), dims[axis_at] // parts).reshape((-1,) + (1,) * (len(dims) - axis_at - 1))

    gain = one(*cuts[0])
    for cut in cuts[1:]:
        gain = gain * one(*cut)
    return gain


def gaussian(stream_key, extent, scale, most, split=(), held_as=jnp.bfloat16):
    drawn = scale * jax.random.normal(stream_key, extent, jnp.float32)
    if split:
        drawn = drawn * steps_of(stream_key, extent, split, -0.22, 0.18)
    return jnp.clip(drawn, -most, most).astype(held_as)


def setup_inputs(seed: int = 0) -> dict:
    streams_of = jax.random.split(jax.random.key(seed), 7)
    front_sizes = draw_front_sizes(jax.random.fold_in(streams_of[6], 71), 0)
    unit_rows = draw_unit_rows(jax.random.fold_in(streams_of[6], 71), 0)
    target_rows = draw_target_rows(jax.random.fold_in(streams_of[6], 71), 0)
    leaf_inverse = gaussian(streams_of[3], (N_LEAF * LEAF, LEAF), LEAF ** -0.5, 0.125, ((0, 8),))
    leaf_coupling = gaussian(streams_of[4], (SEPSUM, N_LEAF * LEAF), 0.1, 0.59765625, ((1, 8),))
    sep_factor = draw_sep_factor(jax.random.fold_in(streams_of[6], 71), 0)
    return {"front_sizes": front_sizes, "unit_rows": unit_rows, "target_rows": target_rows, "leaf_inverse": leaf_inverse, "leaf_coupling": leaf_coupling, "sep_factor": sep_factor}


def level_layout(level_count, unit):
    widths = [0] + [unit * 2 ** (level - 1) for level in range(1, level_count + 1)]
    starts = [0] * (level_count + 1)
    running = 0
    for level in range(1, level_count + 1):
        starts[level] = running
        running += widths[level]
    couplings = {}
    for source in range(1, level_count + 1):
        for ancestor in range(source + 1, level_count + 1):
            couplings[(source, ancestor)] = running
            running += widths[ancestor]
    return widths, starts, couplings


def reference(front_sizes, unit_rows, target_rows, leaf_inverse, leaf_coupling, sep_factor):
    widths, starts, couplings = level_layout(LEVELS, SEP)
    contract = (((0,), (0,)), ((), ()))
    leaves = (unit_rows // LEAF).astype(jnp.int32)
    offsets = (unit_rows - leaves * LEAF).astype(jnp.int32)
    positions = jnp.arange(LEAF, dtype=jnp.int32)

    def leaf_forward(item):
        leaf, offset = item
        column = lax.dynamic_slice(leaf_inverse, (leaf * LEAF, offset), (LEAF, 1))[:, 0]
        live = positions < front_sizes[leaf]
        leaf_y = jnp.where(live, column.astype(jnp.float32), jnp.float32(0.0)).astype(jnp.bfloat16)
        block = lax.dynamic_slice(leaf_coupling, (jnp.int32(0), leaf * LEAF), (SEPSUM, LEAF))
        return leaf_y, jnp.dot(block, leaf_y, preferred_element_type=jnp.float32)

    leaf_y, pushed = lax.map(leaf_forward, (leaves, offsets))

    upward = [None]
    selects = [None]
    for level in range(1, LEVELS + 1):
        blocks = N_LEAF >> level
        select = (jnp.arange(blocks, dtype=jnp.int32)[:, None] == (leaves >> level)[None, :]).astype(jnp.float32)
        selects.append(select)
        portion = pushed[:, starts[level]:starts[level] + widths[level]].T
        upward.append(select[:, None, :] * portion[None, :, :])

    solved = [None] * (LEVELS + 1)
    for level in range(1, LEVELS + 1):
        width = widths[level]
        stored = []
        for index in range(N_LEAF >> level):
            inverse = sep_factor[index * width:(index + 1) * width, starts[level]:starts[level] + width]
            right = (-upward[level][index]).astype(jnp.bfloat16)
            sep_y = jnp.dot(inverse, right, preferred_element_type=jnp.float32).astype(jnp.bfloat16)
            stored.append(sep_y)
            for ancestor in range(level + 1, LEVELS + 1):
                begin = couplings[(level, ancestor)]
                block = sep_factor[index * width:(index + 1) * width, begin:begin + widths[ancestor]]
                update = lax.dot_general(block, sep_y, contract, preferred_element_type=jnp.float32)
                upward[ancestor] = upward[ancestor].at[index >> (ancestor - level)].add(update)
        solved[level] = stored

    settled = [None] * (LEVELS + 1)
    for level in range(LEVELS, 0, -1):
        width = widths[level]
        stored = []
        for index in range(N_LEAF >> level):
            inverse = sep_factor[index * width:(index + 1) * width, starts[level]:starts[level] + width]
            sep_z = solved[level][index].astype(jnp.float32)
            for ancestor in range(level + 1, LEVELS + 1):
                begin = couplings[(level, ancestor)]
                block = sep_factor[index * width:(index + 1) * width, begin:begin + widths[ancestor]]
                sep_z = sep_z - jnp.dot(block, settled[ancestor][index >> (ancestor - level)], preferred_element_type=jnp.float32)
            sep_z = sep_z.astype(jnp.bfloat16)
            stored.append(lax.dot_general(inverse, sep_z, contract, preferred_element_type=jnp.float32).astype(jnp.bfloat16))
        settled[level] = stored

    picked = []
    for level in range(1, LEVELS + 1):
        stacked = jnp.stack(settled[level]).astype(jnp.float32)
        picked.append(jnp.sum(selects[level][:, None, :] * stacked, axis=0).astype(jnp.bfloat16))
    ancestors = jnp.concatenate(picked, axis=0).T

    def leaf_backward(item):
        leaf, column_y, above, targets = item
        block = lax.dynamic_slice(leaf_coupling, (jnp.int32(0), leaf * LEAF), (SEPSUM, LEAF))
        leaf_z = (column_y.astype(jnp.float32) - jnp.dot(above, block, preferred_element_type=jnp.float32)).astype(jnp.bfloat16)
        inverse = lax.dynamic_slice(leaf_inverse, (leaf * LEAF, jnp.int32(0)), (LEAF, LEAF))
        leaf_x = jnp.dot(leaf_z, inverse, preferred_element_type=jnp.float32)
        leaf_x = jnp.where(positions < front_sizes[leaf], leaf_x, jnp.float32(0.0))
        return leaf_x[targets]

    entries = lax.map(leaf_backward, (leaves, leaf_y, ancestors, target_rows.T))
    return entries.T
```

```python
import functools

import jax
import jax.numpy as jnp
from jax import lax
from jax.experimental import pallas as pl
from jax.experimental.pallas import tpu as pltpu
from jax.sharding import PartitionSpec as P

MESH = pl.DeviceIdType.MESH
LANES = 128
LOADS = 4
CHUNKS = 2


def from_partner(x, axis, stride):
    return lax.ppermute(x, axis, [(i, i ^ 1 << stride) for i in range(lax.axis_size(axis))])


def level_layout(level_count, unit):
    widths = [0] + [unit * 2 ** (level - 1) for level in range(1, level_count + 1)]
    starts = [0] * (level_count + 1)
    running = 0
    for level in range(1, level_count + 1):
        starts[level] = running
        running += widths[level]
    couplings = {}
    for source in range(1, level_count + 1):
        for ancestor in range(source + 1, level_count + 1):
            couplings[source, ancestor] = running
            running += widths[ancestor]
    return (widths, starts, couplings)


def many_levels(front_sizes, unit_rows, target_rows, leaf_inverse, leaf_coupling, sep_factor):
    team_count = lax.axis_size("leaf")
    level_count = team_count.bit_length() - 1
    lane_count = lax.axis_size("blk")
    team = lax.axis_index("leaf")
    lane = lax.axis_index("blk")
    own_rows, leaf_width = leaf_inverse.shape
    sep_rows = sep_factor.shape[0]
    widths, starts, couplings = level_layout(level_count, sep_rows * lane_count * 2)
    contract = (((0,), (0,)), ((), ()))

    def block_total(amount, level):
        total = lax.psum(amount, "blk")
        for bit in range(level):
            total = total + from_partner(total, "leaf", bit)
        return total

    front = jnp.sum(jnp.where(jnp.arange(team_count) == team, front_sizes, 0))
    row_index = lane * own_rows + jnp.arange(own_rows)
    live = (row_index < front)[:, None]
    column_leaf = unit_rows // leaf_width
    onehot = (unit_rows[None, :] == team * leaf_width + jnp.arange(leaf_width)[:, None]).astype(
        jnp.bfloat16
    )
    leaf_y = jnp.where(
        live, jnp.dot(leaf_inverse, onehot, preferred_element_type=jnp.float32), 0.0
    ).astype(jnp.bfloat16)
    pushed = jnp.dot(leaf_coupling, leaf_y, preferred_element_type=jnp.float32)
    upward = [None] + [
        pushed[starts[level] : starts[level] + widths[level]] for level in range(1, level_count + 1)
    ]
    solved = [None] * (level_count + 1)
    for level in range(1, level_count + 1):
        total = block_total(upward[level], level)
        right = (-total).astype(jnp.bfloat16)
        inverse = sep_factor[:, starts[level] : starts[level] + widths[level]]
        solved[level] = jnp.dot(inverse, right, preferred_element_type=jnp.float32).astype(
            jnp.bfloat16
        )
        for ancestor in range(level + 1, level_count + 1):
            begin = couplings[level, ancestor]
            block = sep_factor[:, begin : begin + widths[ancestor]]
            upward[ancestor] = upward[ancestor] + lax.dot_general(
                block, solved[level], contract, preferred_element_type=jnp.float32
            )
    settled = [None] * (level_count + 1)
    for level in range(level_count, 0, -1):
        reduced = solved[level].astype(jnp.float32)
        for ancestor in range(level + 1, level_count + 1):
            begin = couplings[level, ancestor]
            block = sep_factor[:, begin : begin + widths[ancestor]]
            reduced = reduced - jnp.dot(
                block, settled[ancestor], preferred_element_type=jnp.float32
            )
        reduced = reduced.astype(jnp.bfloat16)
        inverse = sep_factor[:, starts[level] : starts[level] + widths[level]]
        portion = lax.dot_general(inverse, reduced, contract, preferred_element_type=jnp.float32)
        settled[level] = block_total(portion, level).astype(jnp.bfloat16)
    ancestors = jnp.concatenate(settled[1:], axis=0)
    leaf_z = (
        leaf_y.astype(jnp.float32)
        - lax.dot_general(leaf_coupling, ancestors, contract, preferred_element_type=jnp.float32)
    ).astype(jnp.bfloat16)
    terms = lax.dot_general(leaf_inverse, leaf_z, contract, preferred_element_type=jnp.float32)
    mine = (column_leaf == team)[None, :] & (target_rows < front)
    picks = jnp.where(mine, jnp.take_along_axis(terms, target_rows, axis=0), 0.0)
    return lax.psum_scatter(picks, ("leaf", "blk"), scatter_dimension=0, tiled=True)


def solve_kernel(
    teams,
    lanes,
    front_hbm,
    unit_hbm,
    target_hbm,
    inverse_hbm,
    coupling_hbm,
    sep_hbm,
    out_ref,
    front,
    unit,
    target,
    inverse,
    coupling,
    sep,
    leaf_y,
    whole_sep,
    part,
    part_in,
    half,
    half_in,
    picks,
    picks_in,
    load_sem,
    sep_send,
    sep_recv,
    sum_send,
    sum_recv,
    pick_send,
    pick_recv,
):
    team = lax.axis_index("leaf")
    lane = lax.axis_index("blk")
    place = team * lanes + lane
    rows, width = inverse.shape
    size = coupling.shape[0]
    columns = unit.shape[1]
    own_sep = sep.shape[0]
    out_rows = out_ref.shape[0]
    bits = lanes.bit_length() - 1
    stride = rows // LOADS
    f32, bf16 = jnp.float32, jnp.bfloat16

    def device(other_team, other_lane):
        return {"leaf": other_team, "blk": other_lane}

    others = [(t, k) for t in range(teams) for k in range(lanes) if (t, k) != (0, 0)]

    loads = [
        pltpu.make_async_copy(front_hbm, front, load_sem.at[0]),
        pltpu.make_async_copy(unit_hbm, unit, load_sem.at[1]),
        pltpu.make_async_copy(sep_hbm, sep, load_sem.at[2]),
    ]
    blocks = [
        pltpu.make_async_copy(
            inverse_hbm.at[pl.ds(i * stride, stride)],
            inverse.at[pl.ds(i * stride, stride)],
            load_sem.at[5 + i],
        )
        for i in range(LOADS)
    ]
    later = [
        pltpu.make_async_copy(coupling_hbm, coupling, load_sem.at[3]),
        pltpu.make_async_copy(target_hbm, target, load_sem.at[4]),
    ]
    for copy in loads + blocks + later:
        copy.start()

    barrier = pltpu.get_barrier_semaphore()
    for t, k in others:
        pl.semaphore_signal(
            barrier, inc=1, device_id=device(team ^ t, lane ^ k), device_id_type=MESH
        )

    for copy in loads:
        copy.wait()
    own = pl.ds(pl.multiple_of(place * own_sep, own_sep), own_sep)
    whole_sep[own, :] = sep[...].astype(f32)
    offset = unit[...] - team * width
    onehot = (lax.broadcasted_iota(jnp.int32, (width, columns), 0) == offset).astype(f32).astype(bf16)

    pl.semaphore_wait(barrier, len(others))

    def sep_copy(slot, piece, other_team, other_lane):
        block = pl.ds(pl.multiple_of(piece * own_sep, own_sep), own_sep)
        return pltpu.make_async_remote_copy(
            src_ref=whole_sep.at[block],
            dst_ref=whole_sep.at[block],
            send_sem=sep_send.at[slot],
            recv_sem=sep_recv.at[slot],
            device_id=device(other_team, other_lane),
            device_id_type=MESH,
        )

    wide = [sep_copy(k, place, team, lane ^ k) for k in range(1, lanes)]
    for copy in wide:
        copy.start()
    across = [sep_copy(lanes, place, team ^ 1, lane)]
    across[0].start()

    later[0].wait()
    live_end = front[team] - lane * rows
    pushed = None
    for i in range(LOADS):
        blocks[i].wait()
        block = pl.ds(i * stride, stride)
        values = jnp.dot(inverse[block, :], onehot, preferred_element_type=f32)
        index = lax.broadcasted_iota(jnp.int32, (stride, columns), 0) + i * stride
        values = jnp.where(index < live_end, values, 0.0)
        leaf_y[block, :] = values
        term = jnp.dot(coupling[:, block], values.astype(bf16), preferred_element_type=f32)
        pushed = term if pushed is None else pushed + term
    part[...] = pushed

    chunk = size // (bits * CHUNKS)

    def exchange(step, share, piece, source, target_ref):
        slot = (step * bits + share) * CHUNKS + piece
        block = pl.ds((share * CHUNKS + piece) * chunk, chunk)
        return pltpu.make_async_remote_copy(
            src_ref=source.at[block],
            dst_ref=target_ref.at[block],
            send_sem=sum_send.at[slot],
            recv_sem=sum_recv.at[slot],
            device_id=device(team, lane ^ (1 << (share + step) % bits)),
            device_id_type=MESH,
        )

    order = [(share, piece) for piece in range(CHUNKS) for share in range(bits)]
    sums = [part] + [half.at[i] for i in range(bits - 1)]
    arrive = [part_in] + [half_in.at[i] for i in range(bits - 1)]
    flights = [
        {key: exchange(step, *key, sums[step], arrive[step]) for key in order}
        for step in range(bits)
    ]
    for key in order:
        flights[0][key].start()

    for k in range(1, lanes):
        wide[k - 1].wait_recv()
        copy = sep_copy(lanes + k, team * lanes + (lane ^ k), team ^ 1, lane)
        copy.start()
        across.append(copy)
    later[1].wait()
    y_turned = leaf_y[...].T
    count = target.shape[0]
    padded = jnp.concatenate(
        [target[...], jnp.zeros((LANES - count, columns), jnp.int32)], axis=0
    )
    wanted = padded.T
    low = wanted % LANES
    high = wanted // LANES

    for step in range(1, bits):
        for share, piece in order:
            block = pl.ds((share * CHUNKS + piece) * chunk, chunk)
            flights[step - 1][share, piece].wait_recv()
            sums[step][block, :] = sums[step - 1][block, :] + arrive[step - 1][block, :]
            flights[step][share, piece].start()

    for copy in across:
        copy.wait_recv()
    matrix = whole_sep[...].astype(bf16)

    for key in order:
        flights[bits - 1][key].wait_recv()
    right = (-(sums[bits - 1][...] + arrive[bits - 1][...])).astype(bf16)
    sep_y = jnp.dot(matrix, right, preferred_element_type=f32)
    sep_z = sep_y.T.astype(bf16)
    sep_x = jnp.dot(sep_z, matrix, preferred_element_type=f32).astype(bf16)
    leaf_z = (
        y_turned.astype(bf16).astype(f32)
        - jnp.dot(sep_x, coupling[...], preferred_element_type=f32)
    ).astype(bf16)

    found = jnp.zeros((columns, LANES), f32)
    for i in range(width // LANES):
        terms = jnp.dot(
            leaf_z, inverse[:, i * LANES : (i + 1) * LANES], preferred_element_type=f32
        )
        here = jnp.take_along_axis(terms, low, axis=1)
        found = jnp.where(high == i, here, found)
    mine = (offset >= 0) & (offset < width) & (target[...] < front[team])
    chosen = jnp.where(mine, found.T[:count], 0.0)
    for i in range(teams * lanes):
        picks[i] = chosen[i * out_rows : (i + 1) * out_rows]

    gathers = []
    for i, (t, k) in enumerate(others):
        other = (team ^ t) * lanes + (lane ^ k)
        gathers.append(
            pltpu.make_async_remote_copy(
                src_ref=picks.at[other],
                dst_ref=picks_in.at[i],
                send_sem=pick_send.at[i],
                recv_sem=pick_recv.at[i],
                device_id=device(team ^ t, lane ^ k),
                device_id_type=MESH,
            )
        )
    for copy in gathers:
        copy.start()
    total = picks[place]
    for i, copy in enumerate(gathers):
        copy.wait_recv()
        total = total + picks_in[i]
    out_ref[...] = total

    for copy in wide + across + gathers:
        copy.wait_send()
    for flight in flights:
        for key in order:
            flight[key].wait_send()


def one_level(front_sizes, unit_rows, target_rows, leaf_inverse, leaf_coupling, sep_factor):
    teams = lax.axis_size("leaf")
    lanes = lax.axis_size("blk")
    rows, width = leaf_inverse.shape
    size = leaf_coupling.shape[0]
    columns = unit_rows.shape[0]
    count = target_rows.shape[0]
    group = teams * lanes
    bits = lanes.bit_length() - 1
    f32, bf16 = jnp.float32, jnp.bfloat16
    anywhere = pl.BlockSpec(memory_space=pl.ANY)
    dma = pltpu.SemaphoreType.DMA
    return pl.pallas_call(
        functools.partial(solve_kernel, teams, lanes),
        out_shape=jax.ShapeDtypeStruct((count // group, columns), f32),
        in_specs=[anywhere] * 6,
        out_specs=pl.BlockSpec(memory_space=pltpu.VMEM),
        scratch_shapes=[
            pltpu.SMEM(front_sizes.shape, jnp.int32),
            pltpu.VMEM((1, columns), jnp.int32),
            pltpu.VMEM((count, columns), jnp.int32),
            pltpu.VMEM((rows, width), bf16),
            pltpu.VMEM((size, rows), bf16),
            pltpu.VMEM(sep_factor.shape, bf16),
            pltpu.VMEM((rows, columns), f32),
            pltpu.VMEM((size, size), f32),
            pltpu.VMEM((size, columns), f32),
            pltpu.VMEM((size, columns), f32),
            pltpu.VMEM((bits - 1, size, columns), f32),
            pltpu.VMEM((bits - 1, size, columns), f32),
            pltpu.VMEM((group, count // group, columns), f32),
            pltpu.VMEM((group - 1, count // group, columns), f32),
            dma((5 + LOADS,)),
            dma((2 * lanes,)),
            dma((2 * lanes,)),
            dma((bits * bits * CHUNKS,)),
            dma((bits * bits * CHUNKS,)),
            dma((group - 1,)),
            dma((group - 1,)),
        ],
        compiler_params=pltpu.CompilerParams(collective_id=0, has_side_effects=True),
    )(
        front_sizes,
        unit_rows.reshape(1, columns),
        target_rows,
        leaf_inverse,
        leaf_coupling,
        sep_factor,
    )


def solution(mesh):
    placed = (
        P(),
        P("col"),
        P(None, "col"),
        P(("leaf", "blk"), None),
        P(None, ("leaf", "blk")),
        P(("leaf", "blk"), None),
    )
    body = one_level if mesh.shape["leaf"] == 2 else many_levels
    return jax.shard_map(
        body, mesh=mesh, in_specs=placed, out_specs=P(("leaf", "blk"), "col"), check_vma=False
    )
```

```python
import functools

import jax
import jax.numpy as jnp
from jax import lax
from jax.experimental import pallas as pl
from jax.experimental.pallas import tpu as pltpu
from jax.sharding import PartitionSpec as P

MESH = pl.DeviceIdType.MESH
LANES = 128
LOADS = 4
CHUNKS = 2
WIDE = 256


def from_partner(x, axis, stride):
    return lax.ppermute(x, axis, [(i, i ^ 1 << stride) for i in range(lax.axis_size(axis))])


def level_layout(level_count, unit):
    widths = [0] + [unit * 2 ** (level - 1) for level in range(1, level_count + 1)]
    starts = [0] * (level_count + 1)
    running = 0
    for level in range(1, level_count + 1):
        starts[level] = running
        running += widths[level]
    couplings = {}
    for source in range(1, level_count + 1):
        for ancestor in range(source + 1, level_count + 1):
            couplings[source, ancestor] = running
            running += widths[ancestor]
    return (widths, starts, couplings)


def many_levels(front_sizes, unit_rows, target_rows, leaf_inverse, leaf_coupling, sep_factor):
    team_count = lax.axis_size("leaf")
    level_count = team_count.bit_length() - 1
    lane_count = lax.axis_size("blk")
    team = lax.axis_index("leaf")
    lane = lax.axis_index("blk")
    own_rows, leaf_width = leaf_inverse.shape
    sep_rows = sep_factor.shape[0]
    widths, starts, couplings = level_layout(level_count, sep_rows * lane_count * 2)
    contract = (((0,), (0,)), ((), ()))

    def block_total(amount, level):
        total = lax.psum(amount, "blk")
        for bit in range(level):
            total = total + from_partner(total, "leaf", bit)
        return total

    front = jnp.sum(jnp.where(jnp.arange(team_count) == team, front_sizes, 0))
    row_index = lane * own_rows + jnp.arange(own_rows)
    live = (row_index < front)[:, None]
    column_leaf = unit_rows // leaf_width
    onehot = (unit_rows[None, :] == team * leaf_width + jnp.arange(leaf_width)[:, None]).astype(
        jnp.bfloat16
    )
    leaf_y = jnp.where(
        live, jnp.dot(leaf_inverse, onehot, preferred_element_type=jnp.float32), 0.0
    ).astype(jnp.bfloat16)
    pushed = jnp.dot(leaf_coupling, leaf_y, preferred_element_type=jnp.float32)
    upward = [None] + [
        pushed[starts[level] : starts[level] + widths[level]] for level in range(1, level_count + 1)
    ]
    solved = [None] * (level_count + 1)
    for level in range(1, level_count + 1):
        total = block_total(upward[level], level)
        right = (-total).astype(jnp.bfloat16)
        inverse = sep_factor[:, starts[level] : starts[level] + widths[level]]
        solved[level] = jnp.dot(inverse, right, preferred_element_type=jnp.float32).astype(
            jnp.bfloat16
        )
        for ancestor in range(level + 1, level_count + 1):
            begin = couplings[level, ancestor]
            block = sep_factor[:, begin : begin + widths[ancestor]]
            upward[ancestor] = upward[ancestor] + lax.dot_general(
                block, solved[level], contract, preferred_element_type=jnp.float32
            )
    settled = [None] * (level_count + 1)
    for level in range(level_count, 0, -1):
        reduced = solved[level].astype(jnp.float32)
        for ancestor in range(level + 1, level_count + 1):
            begin = couplings[level, ancestor]
            block = sep_factor[:, begin : begin + widths[ancestor]]
            reduced = reduced - jnp.dot(
                block, settled[ancestor], preferred_element_type=jnp.float32
            )
        reduced = reduced.astype(jnp.bfloat16)
        inverse = sep_factor[:, starts[level] : starts[level] + widths[level]]
        portion = lax.dot_general(inverse, reduced, contract, preferred_element_type=jnp.float32)
        settled[level] = block_total(portion, level).astype(jnp.bfloat16)
    ancestors = jnp.concatenate(settled[1:], axis=0)
    leaf_z = (
        leaf_y.astype(jnp.float32)
        - lax.dot_general(leaf_coupling, ancestors, contract, preferred_element_type=jnp.float32)
    ).astype(jnp.bfloat16)
    terms = lax.dot_general(leaf_inverse, leaf_z, contract, preferred_element_type=jnp.float32)
    mine = (column_leaf == team)[None, :] & (target_rows < front)
    picks = jnp.where(mine, jnp.take_along_axis(terms, target_rows, axis=0), 0.0)
    return lax.psum_scatter(picks, ("leaf", "blk"), scatter_dimension=0, tiled=True)


def solve_kernel(
    teams,
    lanes,
    front_hbm,
    unit_hbm,
    target_hbm,
    inverse_hbm,
    coupling_hbm,
    sep_hbm,
    out_ref,
    front,
    unit,
    target,
    inverse,
    coupling,
    sep,
    leaf_y,
    whole_sep,
    part,
    part_in,
    half,
    half_in,
    picks,
    picks_in,
    load_sem,
    sep_send,
    sep_recv,
    sum_send,
    sum_recv,
    pick_send,
    pick_recv,
):
    team = lax.axis_index("leaf")
    lane = lax.axis_index("blk")
    place = team * lanes + lane
    rows, width = inverse.shape
    size = coupling.shape[0]
    columns = unit.shape[1]
    own_sep = sep.shape[0]
    out_rows = out_ref.shape[0]
    bits = lanes.bit_length() - 1
    stride = width // LOADS
    f32, bf16 = jnp.float32, jnp.bfloat16

    def device(other_team, other_lane):
        return {"leaf": other_team, "blk": other_lane}

    others = [(t, k) for t in range(teams) for k in range(lanes) if (t, k) != (0, 0)]

    loads = [
        pltpu.make_async_copy(front_hbm, front, load_sem.at[0]),
        pltpu.make_async_copy(unit_hbm, unit, load_sem.at[1]),
        pltpu.make_async_copy(sep_hbm, sep, load_sem.at[2]),
    ]
    blocks = [
        pltpu.make_async_copy(
            inverse_hbm.at[:, pl.ds(i * stride, stride)],
            inverse.at[:, pl.ds(i * stride, stride)],
            load_sem.at[5 + i],
        )
        for i in range(LOADS)
    ]
    later = [
        pltpu.make_async_copy(coupling_hbm, coupling, load_sem.at[3]),
        pltpu.make_async_copy(target_hbm, target, load_sem.at[4]),
    ]
    for copy in loads + blocks + later:
        copy.start()

    barrier = pltpu.get_barrier_semaphore()
    for t, k in others:
        pl.semaphore_signal(
            barrier, inc=1, device_id=device(team ^ t, lane ^ k), device_id_type=MESH
        )

    for copy in loads:
        copy.wait()
    own = pl.ds(pl.multiple_of(place * own_sep, own_sep), own_sep)
    whole_sep[own, :] = sep[...].astype(f32)
    offset = unit[...] - team * width
    onehot = (lax.broadcasted_iota(jnp.int32, (width, columns), 0) == offset).astype(f32).astype(bf16)

    pl.semaphore_wait(barrier, len(others))

    def sep_copy(slot, piece, other_team, other_lane):
        block = pl.ds(pl.multiple_of(piece * own_sep, own_sep), own_sep)
        return pltpu.make_async_remote_copy(
            src_ref=whole_sep.at[block],
            dst_ref=whole_sep.at[block],
            send_sem=sep_send.at[slot],
            recv_sem=sep_recv.at[slot],
            device_id=device(other_team, other_lane),
            device_id_type=MESH,
        )

    wide = [sep_copy(k, place, team, lane ^ k) for k in range(1, lanes)]
    for copy in wide:
        copy.start()
    across = [sep_copy(lanes, place, team ^ 1, lane)]
    across[0].start()

    live_end = front[team] - lane * rows
    values = None
    for i in range(LOADS):
        blocks[i].wait()
        block = slice(i * stride, (i + 1) * stride)
        term = jnp.dot(inverse[:, block], onehot[block], preferred_element_type=f32)
        values = term if values is None else values + term
    index = lax.broadcasted_iota(jnp.int32, (rows, columns), 0)
    values = jnp.where(index < live_end, values, 0.0)
    leaf_y[...] = values
    later[0].wait()
    part[...] = jnp.dot(coupling[...], values.astype(bf16), preferred_element_type=f32)

    chunk = size // (bits * CHUNKS)

    def exchange(step, share, piece, source, target_ref):
        slot = (step * bits + share) * CHUNKS + piece
        block = pl.ds((share * CHUNKS + piece) * chunk, chunk)
        return pltpu.make_async_remote_copy(
            src_ref=source.at[block],
            dst_ref=target_ref.at[block],
            send_sem=sum_send.at[slot],
            recv_sem=sum_recv.at[slot],
            device_id=device(team, lane ^ (1 << (share + step) % bits)),
            device_id_type=MESH,
        )

    order = [(share, piece) for piece in range(CHUNKS) for share in range(bits)]
    sums = [part] + [half.at[i] for i in range(bits - 1)]
    arrive = [part_in] + [half_in.at[i] for i in range(bits - 1)]
    flights = [
        {key: exchange(step, *key, sums[step], arrive[step]) for key in order}
        for step in range(bits)
    ]
    for key in order:
        flights[0][key].start()

    for k in range(1, lanes):
        wide[k - 1].wait_recv()
        copy = sep_copy(lanes + k, team * lanes + (lane ^ k), team ^ 1, lane)
        copy.start()
        across.append(copy)
    later[1].wait()
    y_turned = leaf_y[...].T
    count = target.shape[0]
    padded = jnp.concatenate(
        [target[...], jnp.zeros((LANES - count, columns), jnp.int32)], axis=0
    )
    wanted = padded.T
    low = wanted % LANES
    high = wanted // LANES

    for step in range(1, bits):
        for share, piece in order:
            block = pl.ds((share * CHUNKS + piece) * chunk, chunk)
            flights[step - 1][share, piece].wait_recv()
            sums[step][block, :] = sums[step - 1][block, :] + arrive[step - 1][block, :]
            flights[step][share, piece].start()

    for copy in across:
        copy.wait_recv()
    matrix = whole_sep[...].astype(bf16)

    for key in order:
        flights[bits - 1][key].wait_recv()
    right = (-(sums[bits - 1][...] + arrive[bits - 1][...])).astype(bf16)
    sep_y = jnp.dot(matrix, right, preferred_element_type=f32)
    sep_z = sep_y.T.astype(bf16)
    sep_x = jnp.dot(sep_z, matrix, preferred_element_type=f32).astype(bf16)
    leaf_z = (
        y_turned.astype(bf16).astype(f32)
        - jnp.dot(sep_x, coupling[...], preferred_element_type=f32)
    ).astype(bf16)

    found = jnp.zeros((columns, LANES), f32)
    for start in range(0, width, WIDE):
        terms = jnp.dot(leaf_z, inverse[:, start : start + WIDE], preferred_element_type=f32)
        for i in range(WIDE // LANES):
            here = jnp.take_along_axis(terms[:, i * LANES : (i + 1) * LANES], low, axis=1)
            found = jnp.where(high == start // LANES + i, here, found)
    mine = (offset >= 0) & (offset < width) & (target[...] < front[team])
    chosen = jnp.where(mine, found.T[:count], 0.0)
    for i in range(teams * lanes):
        picks[i] = chosen[i * out_rows : (i + 1) * out_rows]

    gathers = []
    for i, (t, k) in enumerate(others):
        other = (team ^ t) * lanes + (lane ^ k)
        gathers.append(
            pltpu.make_async_remote_copy(
                src_ref=picks.at[other],
                dst_ref=picks_in.at[i],
                send_sem=pick_send.at[i],
                recv_sem=pick_recv.at[i],
                device_id=device(team ^ t, lane ^ k),
                device_id_type=MESH,
            )
        )
    for copy in gathers:
        copy.start()
    total = picks[place]
    for i, copy in enumerate(gathers):
        copy.wait_recv()
        total = total + picks_in[i]
    out_ref[...] = total

    for copy in wide + across + gathers:
        copy.wait_send()
    for flight in flights:
        for key in order:
            flight[key].wait_send()


def one_level(front_sizes, unit_rows, target_rows, leaf_inverse, leaf_coupling, sep_factor):
    teams = lax.axis_size("leaf")
    lanes = lax.axis_size("blk")
    rows, width = leaf_inverse.shape
    size = leaf_coupling.shape[0]
    columns = unit_rows.shape[0]
    count = target_rows.shape[0]
    group = teams * lanes
    bits = lanes.bit_length() - 1
    f32, bf16 = jnp.float32, jnp.bfloat16
    anywhere = pl.BlockSpec(memory_space=pl.ANY)
    dma = pltpu.SemaphoreType.DMA
    return pl.pallas_call(
        functools.partial(solve_kernel, teams, lanes),
        out_shape=pltpu.VMEM((count // group, columns), f32),
        in_specs=[anywhere] * 6,
        out_specs=pl.BlockSpec(memory_space=pltpu.VMEM),
        scratch_shapes=[
            pltpu.SMEM(front_sizes.shape, jnp.int32),
            pltpu.VMEM((1, columns), jnp.int32),
            pltpu.VMEM((count, columns), jnp.int32),
            pltpu.VMEM((rows, width), bf16),
            pltpu.VMEM((size, rows), bf16),
            pltpu.VMEM(sep_factor.shape, bf16),
            pltpu.VMEM((rows, columns), f32),
            pltpu.VMEM((size, size), f32),
            pltpu.VMEM((size, columns), f32),
            pltpu.VMEM((size, columns), f32),
            pltpu.VMEM((bits - 1, size, columns), f32),
            pltpu.VMEM((bits - 1, size, columns), f32),
            pltpu.VMEM((group, count // group, columns), f32),
            pltpu.VMEM((group - 1, count // group, columns), f32),
            dma((5 + LOADS,)),
            dma((2 * lanes,)),
            dma((2 * lanes,)),
            dma((bits * bits * CHUNKS,)),
            dma((bits * bits * CHUNKS,)),
            dma((group - 1,)),
            dma((group - 1,)),
        ],
        compiler_params=pltpu.CompilerParams(collective_id=0, has_side_effects=True),
    )(
        front_sizes,
        unit_rows.reshape(1, columns),
        target_rows,
        leaf_inverse,
        leaf_coupling,
        sep_factor,
    )


def solution(mesh):
    placed = (
        P(),
        P("col"),
        P(None, "col"),
        P(("leaf", "blk"), None),
        P(None, ("leaf", "blk")),
        P(("leaf", "blk"), None),
    )
    body = one_level if mesh.shape["leaf"] == 2 else many_levels
    return jax.shard_map(
        body, mesh=mesh, in_specs=placed, out_specs=P(("leaf", "blk"), "col"), check_vma=False
    )
```
